512 devices in a mesh: gx: 4 (over z_lo, core), gy: 4 (over z_hi), gz: 32 (over y, x).
Axes of the slice: x: 4, y: 8, z: 8 (z_hi: 4, z_lo: 2; z = z_hi * 2 + z_lo), core: 2. Of those that a mesh axis runs over, the one named last changes fastest.
Arguments:
- gram_factor: bfloat16 [6144, 384, 384], P(('gx', 'gy', 'gz')), may hold values from -0.3125 to 0.3125
- coupling: bfloat16 [6144, 384, 128], P(('gx', 'gy', 'gz')), may hold values from -0.375 to 0.375
- order_class: int32 [6144], P(('gx', 'gy', 'gz')), may hold values from 0 to 2
- first_moves: int32 [1536], P(('gx', 'gy', 'gz')), may hold values from 0 to 11, as said below
- second_moves: int32 [1536], P(('gx', 'gy', 'gz')), may hold values from 0 to 11, as said below
- trace_index: int32 [6144, 128], P(('gx', 'gy', 'gz')), may hold values from 1 to 322, as said below
- owner_index: int32 [6144, 128], P(('gx', 'gy', 'gz')), may hold values from 0 to 255
- traces: bfloat16 [64, 4, 512, 256], P('gx', 'gy', 'gz'), may hold values from -6 to 6
Outputs:
- applied: float32 [64, 4, 512, 256], P('gx', 'gy', 'gz')
The draws below stay inside these ranges and needn't reach their ends.
Inputs may be any that keep to these rules, and one draw needn't show every extreme that they name: `first_moves`: on each device the 3 entries are distinct slots. `second_moves`: on each device the 3 entries are distinct slots. `trace_index`: never a corner cell of the extended grid.
All inputs are finite; a program needn't handle non-finite values.
Results may differ from the reference program's by a relative error of at most 0.0044.
Values may be sent and summed in bfloat16 or wider, within the bound.
No kernel may reach another device: no remote copies, remote signals or barrier semaphores. Data moves between devices by JAX's collectives and lax.ppermute only.
A program may use at most 64 MiB of HBM per device.

```python
import jax
import jax.numpy as jnp
from jax import lax

W = 384
K = 128
R = 256
FX = 16
FZ = 16
E_DEV = 12
M = 3
NDEV = 512
ELEMS = 6144
NXT = 64
NZT = 512
N_GX = 4
N_GY = 4
N_GZ = 32


def slot_lists(key):
    keys = jax.random.split(key, NDEV)
    picks = jax.vmap(lambda single: jax.random.permutation(single, E_DEV)[:M])(keys)
    return picks.reshape(-1).astype(jnp.int32)


def draw_first_moves(key, part):
    return slot_lists(jax.random.fold_in(key, 1))


def draw_second_moves(key, part):
    return slot_lists(jax.random.fold_in(key, 2))


def draw_trace_index(key, part):
    middle = FX * (FZ + 2)
    choice_cells = jax.random.randint(jax.random.fold_in(key, 3), (NDEV * E_DEV, K), 0, middle + 2 * FZ)
    inner = (1 + choice_cells // (FZ + 2)) * (FZ + 2) + choice_cells % (FZ + 2)
    edge = choice_cells - middle
    edge_row = jnp.where(edge < FZ, 0, FX + 1)
    outer = edge_row * (FZ + 2) + 1 + edge % FZ
    return jnp.where(choice_cells < middle, inner, outer).astype(jnp.int32)


def set_ends(values, stream_key, least, largest):
    longest = values.shape.index(max(values.shape))
    spots = []
    for shift in (0, 1):
        where = [jax.random.randint(jax.random.fold_in(stream_key, axis), (), 0, length) for axis, length in enumerate(values.shape)]
        where[longest] = (where[longest] + shift) % values.shape[longest]
        spots.append(tuple(where))
    return values.at[spots[0]].set(least).at[spots[1]].set(largest)


def levels(stream_key, shape, pieces, low, top_value):
    loudness, own = 1.0, jax.random.fold_in(stream_key, 6)
    for dim, parts in pieces:
        draws = jnp.exp(jax.random.uniform(jax.random.fold_in(own, dim), (parts,), jnp.float32, low / len(pieces), top_value / len(pieces)))
        loudness = loudness * jnp.repeat(draws, shape[dim] // parts).reshape([-1 if axis == dim else 1 for axis in range(len(shape))])
    return loudness


def normal_values(key, shape, width, reach, pieces=(), kind=jnp.bfloat16):
    level = levels(key, shape, pieces, -0.22, 0.18) if pieces else 1.0
    drawn = jax.random.normal(key, shape, jnp.float32) * width * level
    return jnp.minimum(jnp.maximum(drawn, -reach), reach).astype(kind)


def setup_inputs(seed: int = 0) -> dict:
    key_list = jax.random.split(jax.random.key(seed), 9)
    gram_factor = normal_values(key_list[0], (ELEMS, W, W), W ** -0.5, 0.3125, ((0, 512),))
    coupling = normal_values(key_list[1], (ELEMS, W, K), (2 * K) ** -0.5, 0.375, ((0, 512),))
    order_class = set_ends(jax.random.randint(key_list[2], (ELEMS,), 0, 3), jax.random.fold_in(key_list[2], 1), 0, 2).astype(jnp.int32)
    first_moves = draw_first_moves(jax.random.fold_in(key_list[8], 71), 0)
    second_moves = draw_second_moves(jax.random.fold_in(key_list[8], 71), 0)
    trace_index = draw_trace_index(jax.random.fold_in(key_list[8], 71), 0)
    owner_index = set_ends(jax.random.randint(key_list[6], (ELEMS, K), 0, FX * FZ), jax.random.fold_in(key_list[6], 1), 0, (FX * FZ) - 1).astype(jnp.int32)
    traces = normal_values(key_list[7], (NXT, N_GY, NZT, R), 1.0, 6.0, ((0, 4), (1, 4), (2, 32)))
    return dict(gram_factor=gram_factor, coupling=coupling, order_class=order_class, first_moves=first_moves, second_moves=second_moves, trace_index=trace_index, owner_index=owner_index, traces=traces)


def element_products(gram_factor, coupling, order_class):
    rows = jnp.arange(W, dtype=jnp.int32)
    widths = (W * (2 + order_class)) // 4
    keep = (rows[None, :] < widths[:, None]).astype(gram_factor.dtype)
    masked = gram_factor * keep[:, :, None]
    def one_element(pair):
        return jnp.dot(pair[0], pair[1], preferred_element_type=jnp.float32).astype(jnp.bfloat16)
    return lax.map(one_element, (masked, coupling))


def relocate(first_moves, second_moves):
    device_ids = jnp.arange(NDEV, dtype=jnp.int32)
    layout = jnp.arange(NDEV * E_DEV, dtype=jnp.int32).reshape(NDEV, E_DEV)
    first_slots = first_moves.reshape(NDEV, M)
    partner = device_ids ^ 1
    layout = layout.at[device_ids[:, None], first_slots].set(layout[partner[:, None], first_slots[partner]])
    second_slots = second_moves.reshape(NDEV, M)
    partner = device_ids ^ N_GZ
    layout = layout.at[device_ids[:, None], second_slots].set(layout[partner[:, None], second_slots[partner]])
    return layout.reshape(-1)


def apply_all(field, operator, trace_index, owner_index):
    padded = jnp.pad(field, ((1, 1), (0, 0), (1, 1), (0, 0)))
    operator = operator.reshape(NDEV, E_DEV, W, K)
    reads = trace_index.reshape(NDEV, E_DEV, K)
    writes = owner_index.reshape(NDEV, E_DEV, K)
    def one_device(device):
        ix = device // (N_GY * N_GZ)
        iy = (device // N_GZ) % N_GY
        iz = device % N_GZ
        block = lax.dynamic_slice(padded, (ix * FX, iy, iz * FZ, jnp.int32(0)), (FX + 2, 1, FZ + 2, R))
        flattened = block.reshape((FX + 2) * (FZ + 2), R)
        gathered = flattened[reads[device]].astype(jnp.float32)
        local_ops = operator[device].astype(jnp.float32)
        tested = jnp.einsum('ewk,ekr->ewr', local_ops, gathered).astype(jnp.bfloat16)
        element_out = jnp.einsum('ewk,ewr->ekr', local_ops, tested.astype(jnp.float32))
        result = jnp.zeros((FX * FZ, R), jnp.float32).at[writes[device].reshape(-1)].add(element_out.reshape(-1, R))
        return result
    blocks = lax.map(one_device, jnp.arange(NDEV, dtype=jnp.int32))
    blocks = blocks.reshape(N_GX, N_GY, N_GZ, FX, FZ, R).transpose(0, 3, 1, 2, 4, 5)
    return blocks.reshape(N_GX * FX, N_GY, N_GZ * FZ, R)


def reference(gram_factor, coupling, order_class, first_moves, second_moves, trace_index, owner_index, traces):
    operator = element_products(gram_factor, coupling, order_class)
    operator = operator[relocate(first_moves, second_moves)]
    first = apply_all(traces, operator, trace_index, owner_index).astype(jnp.bfloat16)
    return apply_all(first, operator, trace_index, owner_index)
```

```python
import functools

import jax
import jax.numpy as jnp
from jax import lax
from jax.experimental import pallas as pl
from jax.experimental.pallas import tpu as pltpu
from jax.sharding import PartitionSpec as P

BF16 = jnp.bfloat16
F32 = jnp.float32
I32 = jnp.int32
HBM = pl.BlockSpec(memory_space=pltpu.MemorySpace.HBM)
VMEM = pl.BlockSpec(memory_space=pltpu.MemorySpace.VMEM)
SMEM = pl.BlockSpec(memory_space=pltpu.MemorySpace.SMEM)


def params(mebibytes):
    return pltpu.CompilerParams(vmem_limit_bytes=mebibytes << 20)


def swap_route(count, bit):
    return [(low, low ^ (1 << bit)) for low in range(count) if low ^ (1 << bit) < count]


def dot(a, b, dims):
    return lax.dot_general(a, b, (dims, ((), ())), preferred_element_type=F32)


def halves(value):
    high = value.astype(BF16)
    return high, (value - high.astype(F32)).astype(BF16)


def gram_of(factor, coupling, order):
    rows = factor.shape[0]
    product = dot(factor, coupling, ((1,), (0,)))
    keep = lax.broadcasted_iota(I32, product.shape, 0) < rows * (2 + order) // 4
    operator = jnp.where(keep, product, 0.0).astype(BF16)
    return dot(operator, operator, ((0,), (0,)))


def one_hot(index, rows):
    hit = lax.broadcasted_iota(I32, (rows, index.shape[1]), 0) == index
    return jnp.where(hit, 1.0, 0.0).astype(BF16)


def cell_of(cell, fx, fz):
    pitch = fz + 2
    row = jnp.zeros_like(cell)
    for edge in range(1, fx + 2):
        row = row + jnp.where(cell >= edge * pitch, 1, 0)
    column = cell - row * pitch
    own = fx * fz
    out = (row - 1) * fz + column - 1
    out = jnp.where(column == fz + 1, own + 2 * fz + fx + row - 1, out)
    out = jnp.where(column == 0, own + 2 * fz + row - 1, out)
    out = jnp.where(row == fx + 1, own + fz + column - 1, out)
    return jnp.where(row == 0, own + column - 1, out)


def matrix_of(elements, own, padded):
    left, right = [], []
    for gram, reads, writes in elements:
        scatter, gather = one_hot(writes, own), one_hot(reads, padded)
        if gram.dtype == F32:
            spread = sum(dot(scatter, half, ((1,), (0,))) for half in halves(gram))
            parts = halves(spread)
        else:
            parts = [dot(scatter, gram, ((1,), (0,))).astype(BF16)]
        left += parts
        right += [gather] * len(parts)
    return dot(jnp.concatenate(left, axis=1), jnp.concatenate(right, axis=1), ((1,), (1,)))


def given_kernel(f, s, order, factor, coupling, given_f, given_s, fbuf, cbuf, sem):
    moves = f.shape[0]
    slots = [f[i] for i in range(moves)] + [s[i] for i in range(moves)]
    copies = []
    for i, slot in enumerate(slots):
        pair = (
            pltpu.make_async_copy(factor.at[slot], fbuf.at[i], sem.at[i, 0]),
            pltpu.make_async_copy(coupling.at[slot], cbuf.at[i], sem.at[i, 1]),
        )
        for copy in pair:
            copy.start()
        copies.append(pair)
    for i, slot in enumerate(slots):
        for copy in copies[i]:
            copy.wait()
        out = given_f if i < moves else given_s
        out[i % moves] = gram_of(fbuf[i], cbuf[i], order[slot]).astype(BF16)


def store_edges(field, edges, fx, fz):
    last, first, right, left = edges
    own = fx * fz
    last[...] = field[own - fz :, :]
    first[...] = field[:fz, :]
    row = lax.broadcasted_iota(I32, (2 * fx, own), 0)
    wanted = jnp.where(row < fx, row * fz + fz - 1, (row - fx) * fz)
    hit = lax.broadcasted_iota(I32, (2 * fx, own), 1) == wanted
    sides = dot(jnp.where(hit, 1.0, 0.0).astype(BF16), field, ((1,), (0,))).astype(BF16)
    right[...] = sides[:fx]
    left[...] = sides[fx:]


def kept_kernel(
    fx, fz, f, s, order, reads, writes, factor, coupling, traces,
    part, e0, e1, e2, e3, fbuf, cbuf, kept, sem,
):
    slots, moves = reads.shape[0], f.shape[0]
    most = slots - moves
    for i in range(slots):
        kept[i] = 0
    count = jnp.int32(0)
    for slot in range(slots):
        moved = f[0] == slot
        for i in range(moves):
            moved = moved | (f[i] == slot) | (s[i] == slot)
        kept[count] = slot
        count = count + jnp.where(moved, 0, 1)
    copies = []
    for i in range(most):
        slot = kept[i]
        pair = (
            pltpu.make_async_copy(factor.at[slot], fbuf.at[i], sem.at[i, 0]),
            pltpu.make_async_copy(coupling.at[slot], cbuf.at[i], sem.at[i, 1]),
        )
        for copy in pair:
            copy.start()
        copies.append(pair)
    store_edges(traces[...], (e0, e1, e2, e3), fx, fz)
    elements = []
    for i in range(most):
        slot = kept[i]
        valid = i < count
        read = jnp.where(valid, cell_of(reads[pl.ds(slot, 1), :], fx, fz), -1)
        write = jnp.where(valid, writes[pl.ds(slot, 1), :], -1)
        for copy in copies[i]:
            copy.wait()
        elements.append((gram_of(fbuf[i], cbuf[i], order[slot]), read, write))
    part[...] = matrix_of(elements, fx * fz, part.shape[1])


def relay_kernel(f, s, given_s, got, out):
    moves = f.shape[0]
    for i in range(moves):
        value = given_s[i]
        for j in range(moves):
            value = jnp.where(s[i] == f[j], got[j], value)
        out[i] = value


def halo_dot(parts, field, halos, own):
    frame = jnp.concatenate([halo[...] for halo in halos], axis=0)
    total = 0.0
    for part in parts:
        total = total + dot(part[:, :own], field, ((1,), (0,)))
        total = total + dot(part[:, own : own + frame.shape[0]], frame, ((1,), (0,)))
    return total


def first_kernel(
    fx, fz, f, s, reads, writes, got_f, got_s, part, traces, h0, h1, h2, h3,
    matrix, first, e0, e1, e2, e3,
):
    own, moves = fx * fz, f.shape[0]
    elements = []
    for i in range(moves):
        slot = s[i]
        read = cell_of(reads[pl.ds(slot, 1), :], fx, fz)
        elements.append((got_s[i], read, writes[pl.ds(slot, 1), :]))
    for i in range(moves):
        slot = f[i]
        stays = slot != s[0]
        for j in range(1, moves):
            stays = stays & (slot != s[j])
        read = jnp.where(stays, cell_of(reads[pl.ds(slot, 1), :], fx, fz), -1)
        write = jnp.where(stays, writes[pl.ds(slot, 1), :], -1)
        elements.append((got_f[i], read, write))
    whole = part[...] + matrix_of(elements, own, part.shape[1])
    parts = halves(whole)
    matrix[0], matrix[1] = parts
    field = halo_dot(parts, traces[...], (h0, h1, h2, h3), own).astype(BF16)
    first[...] = field
    store_edges(field, (e0, e1, e2, e3), fx, fz)


def second_kernel(own, matrix, first, h0, h1, h2, h3, out):
    out[...] = halo_dot((matrix[0], matrix[1]), first[...], (h0, h1, h2, h3), own)


def exchange(edges):
    last, first, right, left = edges
    out = []
    for axis, up, down in (("gx", last, first), ("gz", right, left)):
        count = lax.axis_size(axis)
        forward = [(i, i + 1) for i in range(count - 1)]
        backward = [(target, source) for source, target in forward]
        out += [lax.ppermute(up, axis, forward), lax.ppermute(down, axis, backward)]
    return out


def body(
    gram_factor, coupling, order_class, first_moves, second_moves, trace_index, owner_index, traces
):
    slots, width, unknowns = coupling.shape
    moves = first_moves.shape[0]
    fx, _, fz, columns = traces.shape
    own = fx * fz
    padded = -(-(own + 2 * (fx + fz)) // 128) * 128
    most = slots - moves
    field = traces.reshape(own, columns)
    grams = jax.ShapeDtypeStruct((moves, unknowns, unknowns), BF16)
    edges = [jax.ShapeDtypeStruct((n, columns), BF16) for n in (fz, fz, fx, fx)]

    given_f, given_s = pl.pallas_call(
        given_kernel,
        out_shape=(grams, grams),
        in_specs=[SMEM] * 3 + [HBM] * 2,
        out_specs=(VMEM, VMEM),
        scratch_shapes=[
            pltpu.VMEM((2 * moves, width, width), BF16),
            pltpu.VMEM((2 * moves, width, unknowns), BF16),
            pltpu.SemaphoreType.DMA((2 * moves, 2)),
        ],
        compiler_params=params(53),
        name="given",
    )(first_moves, second_moves, order_class, gram_factor, coupling)

    given_f, given_s, field = lax.optimization_barrier((given_f, given_s, field))
    got_f = lax.ppermute(given_f, "gz", swap_route(lax.axis_size("gz"), 0))

    part, *trace_edges = pl.pallas_call(
        functools.partial(kept_kernel, fx, fz),
        out_shape=(jax.ShapeDtypeStruct((own, padded), F32), *edges),
        in_specs=[SMEM] * 3 + [VMEM] * 2 + [HBM] * 2 + [VMEM],
        out_specs=(VMEM,) * 5,
        scratch_shapes=[
            pltpu.VMEM((most, width, width), BF16),
            pltpu.VMEM((most, width, unknowns), BF16),
            pltpu.SMEM((slots,), I32),
            pltpu.SemaphoreType.DMA((most, 2)),
        ],
        cost_estimate=pl.CostEstimate(
            flops=2 * most * width * unknowns * (width + unknowns),
            bytes_accessed=2 * most * width * (width + unknowns),
            transcendentals=0,
        ),
        compiler_params=params(53),
        name="kept",
    )(
        first_moves, second_moves, order_class, trace_index, owner_index,
        gram_factor, coupling, field,
    )

    given_s, part = lax.optimization_barrier((given_s, part))
    relayed = pl.pallas_call(
        relay_kernel,
        out_shape=grams,
        in_specs=[SMEM] * 2 + [VMEM] * 2,
        out_specs=VMEM,
        compiler_params=params(2),
        name="relay",
    )(first_moves, second_moves, given_s, got_f)
    both = lax.axis_size("gy") * lax.axis_size("gz")
    second_bit = lax.axis_size("gz").bit_length() - 1
    got_s = lax.ppermute(relayed, ("gy", "gz"), swap_route(both, second_bit))

    halos = exchange(trace_edges)
    matrix, first, *first_edges = pl.pallas_call(
        functools.partial(first_kernel, fx, fz),
        out_shape=(
            jax.ShapeDtypeStruct((2, own, padded), BF16),
            jax.ShapeDtypeStruct((own, columns), BF16),
            *edges,
        ),
        in_specs=[SMEM] * 2 + [VMEM] * 10,
        out_specs=(VMEM,) * 6,
        compiler_params=params(12),
        name="first",
    )(
        first_moves, second_moves, trace_index, owner_index, got_f, got_s, part, field, *halos
    )

    halos = exchange(first_edges)
    second = pl.pallas_call(
        functools.partial(second_kernel, own),
        out_shape=jax.ShapeDtypeStruct((own, columns), F32),
        in_specs=[VMEM] * 6,
        out_specs=VMEM,
        compiler_params=params(6),
        name="second",
    )(matrix, first, *halos)
    return second.reshape(traces.shape)


def solution(mesh):
    return jax.shard_map(
        body,
        mesh=mesh,
        in_specs=(
            P(("gx", "gy", "gz"), None, None),
            P(("gx", "gy", "gz"), None, None),
            P(("gx", "gy", "gz")),
            P(("gx", "gy", "gz")),
            P(("gx", "gy", "gz")),
            P(("gx", "gy", "gz"), None),
            P(("gx", "gy", "gz"), None),
            P("gx", "gy", "gz", None),
        ),
        out_specs=P("gx", "gy", "gz", None),
        check_vma=False,
    )
```

```python
import functools

import jax
import jax.numpy as jnp
from jax import lax
from jax.experimental import pallas as pl
from jax.experimental.pallas import tpu as pltpu
from jax.sharding import PartitionSpec as P

BF16 = jnp.bfloat16
F32 = jnp.float32
I32 = jnp.int32
HBM = pl.BlockSpec(memory_space=pltpu.MemorySpace.HBM)
VMEM = pl.BlockSpec(memory_space=pltpu.MemorySpace.VMEM)
SMEM = pl.BlockSpec(memory_space=pltpu.MemorySpace.SMEM)


def params(mebibytes):
    return pltpu.CompilerParams(vmem_limit_bytes=mebibytes << 20)


def swap_route(count, bit):
    return [(low, low ^ (1 << bit)) for low in range(count) if low ^ (1 << bit) < count]


def dot(a, b, dims):
    return lax.dot_general(a, b, (dims, ((), ())), preferred_element_type=F32)


def halves(value):
    high = value.astype(BF16)
    return high, (value - high.astype(F32)).astype(BF16)


def gram_of(factor, coupling, order):
    rows = factor.shape[0]
    product = dot(factor, coupling, ((1,), (0,)))
    keep = lax.broadcasted_iota(I32, product.shape, 0) < rows * (2 + order) // 4
    operator = jnp.where(keep, product, 0.0).astype(BF16)
    return dot(operator, operator, ((0,), (0,)))


def one_hot(index, rows):
    hit = lax.broadcasted_iota(I32, (rows, index.shape[1]), 0) == index
    return jnp.where(hit, 1.0, 0.0).astype(BF16)


def parities():
    return lax.axis_index("gx") % 2, lax.axis_index("gz") % 2


def cell_of(cell, fx, fz):
    odd_x, odd_z = parities()
    pitch = fz + 2
    row = jnp.zeros_like(cell)
    for edge in range(1, fx + 2):
        row = row + jnp.where(cell >= edge * pitch, 1, 0)
    column = cell - row * pitch
    base_x = fx * fz
    base_z = base_x + 2 * fz
    out = (row - 1) * fz + column - 1
    out = jnp.where(column == fz + 1, base_z + odd_z * fx + row - 1, out)
    out = jnp.where(column == 0, base_z + (1 - odd_z) * fx + row - 1, out)
    out = jnp.where(row == fx + 1, base_x + odd_x * fz + column - 1, out)
    return jnp.where(row == 0, base_x + (1 - odd_x) * fz + column - 1, out)


def edges_of(field, fx, fz):
    odd_x, odd_z = parities()
    own = fx * fz
    last, first = field[own - fz :, :], field[:fz, :]
    row = lax.broadcasted_iota(I32, (2 * fx, own), 0)
    wanted = jnp.where(row < fx, row * fz + fz - 1, (row - fx) * fz)
    hit = lax.broadcasted_iota(I32, (2 * fx, own), 1) == wanted
    sides = dot(jnp.where(hit, 1.0, 0.0).astype(BF16), field, ((1,), (0,)))
    right, left = sides[:fx], sides[fx:]
    flip_x, flip_z = odd_x == 1, odd_z == 1
    return (
        jnp.where(flip_x, first, last),
        jnp.where(flip_x, last, first),
        jnp.where(flip_z, left, right).astype(BF16),
        jnp.where(flip_z, right, left).astype(BF16),
    )


def matrix_of(elements, own, padded):
    left, right = [], []
    for gram, reads, writes in elements:
        scatter, gather = one_hot(writes, own), one_hot(reads, padded)
        if gram.dtype == F32:
            spread = sum(dot(scatter, half, ((1,), (0,))) for half in halves(gram))
            parts = halves(spread)
        else:
            parts = [dot(scatter, gram, ((1,), (0,))).astype(BF16)]
        left += parts
        right += [gather] * len(parts)
    return dot(jnp.concatenate(left, axis=1), jnp.concatenate(right, axis=1), ((1,), (1,)))


def fetch(slots, factor, coupling, fbuf, cbuf, sem):
    copies = []
    for i, slot in enumerate(slots):
        pair = (
            pltpu.make_async_copy(factor.at[slot], fbuf.at[i], sem.at[i, 0]),
            pltpu.make_async_copy(coupling.at[slot], cbuf.at[i], sem.at[i, 1]),
        )
        for copy in pair:
            copy.start()
        copies.append(pair)
    return copies


def given_kernel(
    fx, fz, moves, with_edges, f, order, factor, coupling, *rest
):
    if with_edges:
        traces, out, e0, e1, e3, fbuf, cbuf, sem = rest
    else:
        out, fbuf, cbuf, sem = rest
    slots = [f[i] for i in range(moves)]
    copies = fetch(slots, factor, coupling, fbuf, cbuf, sem)
    unknowns = coupling.shape[2]
    if with_edges:
        field = traces[...]
        e0[...], e1[...], side, e3[...] = edges_of(field, fx, fz)
        for i in range(field.shape[1] // unknowns):
            out[pl.ds(moves * unknowns + i * fx, fx), :] = side[:, i * unknowns : (i + 1) * unknowns]
    for i, slot in enumerate(slots):
        for copy in copies[i]:
            copy.wait()
        gram = gram_of(fbuf[i], cbuf[i], order[slot])
        out[pl.ds(i * unknowns, unknowns), :] = gram.astype(BF16)


def kept_kernel(fx, fz, f, s, order, reads, writes, factor, coupling, part, fbuf, cbuf, kept, sem):
    slots, moves = reads.shape[0], f.shape[0]
    most = slots - moves
    for i in range(slots):
        kept[i] = 0
    count = jnp.int32(0)
    for slot in range(slots):
        moved = f[0] == slot
        for i in range(moves):
            moved = moved | (f[i] == slot) | (s[i] == slot)
        kept[count] = slot
        count = count + jnp.where(moved, 0, 1)
    slots = [kept[i] for i in range(most)]
    copies = fetch(slots, factor, coupling, fbuf, cbuf, sem)
    elements = []
    for i, slot in enumerate(slots):
        valid = i < count
        read = jnp.where(valid, cell_of(reads[pl.ds(slot, 1), :], fx, fz), -1)
        write = jnp.where(valid, writes[pl.ds(slot, 1), :], -1)
        for copy in copies[i]:
            copy.wait()
        elements.append((gram_of(fbuf[i], cbuf[i], order[slot]), read, write))
    part[...] = matrix_of(elements, fx * fz, part.shape[1])


def relay_kernel(f, s, given, got, out):
    moves = f.shape[0]
    unknowns = given.shape[0] // moves
    for i in range(moves):
        value = given[pl.ds(i * unknowns, unknowns), :]
        for j in range(moves):
            value = jnp.where(s[i] == f[j], got[pl.ds(j * unknowns, unknowns), :], value)
        out[pl.ds(i * unknowns, unknowns), :] = value


def halo_dot(parts, field, frame, own):
    total = 0.0
    for part in parts:
        total = total + dot(part[:, :own], field, ((1,), (0,)))
        total = total + dot(part[:, own : own + frame.shape[0]], frame, ((1,), (0,)))
    return total


def first_kernel(
    fx, fz, f, s, reads, writes, got, got_s, part, traces, h0, h1, h3,
    matrix, first, e0, e1, e2, e3,
):
    own, moves = fx * fz, f.shape[0]
    unknowns = reads.shape[1]
    columns = traces.shape[1]
    elements = []
    for i in range(moves):
        slot = s[i]
        read = cell_of(reads[pl.ds(slot, 1), :], fx, fz)
        gram = got_s[pl.ds(i * unknowns, unknowns), :]
        elements.append((gram, read, writes[pl.ds(slot, 1), :]))
    for i in range(moves):
        slot = f[i]
        stays = slot != s[0]
        for j in range(1, moves):
            stays = stays & (slot != s[j])
        read = jnp.where(stays, cell_of(reads[pl.ds(slot, 1), :], fx, fz), -1)
        write = jnp.where(stays, writes[pl.ds(slot, 1), :], -1)
        elements.append((got[pl.ds(i * unknowns, unknowns), :], read, write))
    whole = part[...] + matrix_of(elements, own, part.shape[1])
    parts = halves(whole)
    matrix[0], matrix[1] = parts
    side = [
        got[pl.ds(moves * unknowns + i * fx, fx), :] for i in range(columns // unknowns)
    ]
    side = jnp.concatenate(side, axis=1)
    frame = jnp.concatenate([h0[...], h1[...], side, h3[...]], axis=0)
    field = halo_dot(parts, traces[...], frame, own).astype(BF16)
    first[...] = field
    e0[...], e1[...], e2[...], e3[...] = edges_of(field, fx, fz)


def second_kernel(own, matrix, first, h0, h1, h2, h3, out):
    frame = jnp.concatenate([h0[...], h1[...], h2[...], h3[...]], axis=0)
    out[...] = halo_dot((matrix[0], matrix[1]), first[...], frame, own)


def pairs(count, odd):
    route = []
    for low in range(odd, count - 1, 2):
        route += [(low, low + 1), (low + 1, low)]
    return route


def swapped(edge, axis, odd):
    return lax.ppermute(edge, axis, pairs(lax.axis_size(axis), odd))


def body(
    gram_factor, coupling, order_class, first_moves, second_moves, trace_index, owner_index, traces
):
    slots, width, unknowns = coupling.shape
    moves = first_moves.shape[0]
    fx, _, fz, columns = traces.shape
    own = fx * fz
    padded = -(-(own + 2 * (fx + fz)) // 128) * 128
    most = slots - moves
    field = traces.reshape(own, columns)
    grams = jax.ShapeDtypeStruct((moves * unknowns, unknowns), BF16)
    load = jax.ShapeDtypeStruct((moves * unknowns + fx * columns // unknowns, unknowns), BF16)
    edges = [jax.ShapeDtypeStruct((n, columns), BF16) for n in (fz, fz, fx, fx)]

    def element_cost(count):
        return pl.CostEstimate(
            flops=2 * count * width * unknowns * (width + unknowns),
            bytes_accessed=2 * count * width * (width + unknowns),
            transcendentals=0,
        )

    def buffers(count):
        return [
            pltpu.VMEM((count, width, width), BF16),
            pltpu.VMEM((count, width, unknowns), BF16),
        ]

    given, t0, t1, t3 = pl.pallas_call(
        functools.partial(given_kernel, fx, fz, moves, True),
        out_shape=(load, edges[0], edges[1], edges[3]),
        in_specs=[SMEM] * 2 + [HBM] * 2 + [VMEM],
        out_specs=(VMEM,) * 4,
        scratch_shapes=[*buffers(moves), pltpu.SemaphoreType.DMA((moves, 2))],
        compiler_params=params(53),
        cost_estimate=element_cost(moves),
        name="given",
    )(first_moves, order_class, gram_factor, coupling, field)
    given, t0, t1, t3, second_moves = lax.optimization_barrier((given, t0, t1, t3, second_moves))
    got = swapped(given, "gz", 0)

    given_s = pl.pallas_call(
        functools.partial(given_kernel, fx, fz, moves, False),
        out_shape=grams,
        in_specs=[SMEM] * 2 + [HBM] * 2,
        out_specs=VMEM,
        scratch_shapes=[*buffers(moves), pltpu.SemaphoreType.DMA((moves, 2))],
        compiler_params=params(53),
        cost_estimate=element_cost(moves),
        name="passed",
    )(second_moves, order_class, gram_factor, coupling)

    given_s, t3 = lax.optimization_barrier((given_s, t3))
    h3 = swapped(t3, "gz", 1)

    relayed = pl.pallas_call(
        relay_kernel,
        out_shape=grams,
        in_specs=[SMEM] * 2 + [VMEM] * 2,
        out_specs=VMEM,
        compiler_params=params(2),
        name="relay",
    )(first_moves, second_moves, given_s, got)
    relayed, t0, t1, order_class = lax.optimization_barrier((relayed, t0, t1, order_class))
    both = lax.axis_size("gy") * lax.axis_size("gz")
    second_bit = lax.axis_size("gz").bit_length() - 1
    got_s = lax.ppermute(relayed, ("gy", "gz"), swap_route(both, second_bit))
    h1 = swapped(t1, "gx", 1)
    h0 = swapped(t0, "gx", 0)

    part = pl.pallas_call(
        functools.partial(kept_kernel, fx, fz),
        out_shape=jax.ShapeDtypeStruct((own, padded), F32),
        in_specs=[SMEM] * 3 + [VMEM] * 2 + [HBM] * 2,
        out_specs=VMEM,
        scratch_shapes=[
            *buffers(most), pltpu.SMEM((slots,), I32), pltpu.SemaphoreType.DMA((most, 2))
        ],
        compiler_params=params(53),
        cost_estimate=element_cost(most),
        name="kept",
    )(
        first_moves, second_moves, order_class, trace_index, owner_index, gram_factor, coupling
    )

    matrix, first, *first_edges = pl.pallas_call(
        functools.partial(first_kernel, fx, fz),
        out_shape=(
            jax.ShapeDtypeStruct((2, own, padded), BF16),
            jax.ShapeDtypeStruct((own, columns), BF16),
            *edges,
        ),
        in_specs=[SMEM] * 2 + [VMEM] * 9,
        out_specs=(VMEM,) * 6,
        compiler_params=params(12),
        name="first",
    )(
        first_moves, second_moves, trace_index, owner_index, got, got_s, part, field, h0, h1, h3
    )

    e0, e1, e2, e3 = first_edges
    h1 = swapped(e1, "gx", 1)
    h2 = swapped(e2, "gz", 0)
    h3 = swapped(e3, "gz", 1)
    h0 = swapped(e0, "gx", 0)
    second = pl.pallas_call(
        functools.partial(second_kernel, own),
        out_shape=jax.ShapeDtypeStruct((own, columns), F32),
        in_specs=[VMEM] * 6,
        out_specs=VMEM,
        compiler_params=params(6),
        name="second",
    )(matrix, first, h0, h1, h2, h3)
    return second.reshape(traces.shape)


def solution(mesh):
    return jax.shard_map(
        body,
        mesh=mesh,
        in_specs=(
            P(("gx", "gy", "gz"), None, None),
            P(("gx", "gy", "gz"), None, None),
            P(("gx", "gy", "gz")),
            P(("gx", "gy", "gz")),
            P(("gx", "gy", "gz")),
            P(("gx", "gy", "gz"), None),
            P(("gx", "gy", "gz"), None),
            P("gx", "gy", "gz", None),
        ),
        out_specs=P("gx", "gy", "gz", None),
        check_vma=False,
    )
```

```python
import functools

import jax
import jax.numpy as jnp
from jax import lax
from jax.experimental import pallas as pl
from jax.experimental.pallas import tpu as pltpu
from jax.sharding import PartitionSpec as P

BF16 = jnp.bfloat16
F32 = jnp.float32
I32 = jnp.int32
HBM = pl.BlockSpec(memory_space=pltpu.MemorySpace.HBM)
VMEM = pl.BlockSpec(memory_space=pltpu.MemorySpace.VMEM)
SMEM = pl.BlockSpec(memory_space=pltpu.MemorySpace.SMEM)


def params(mebibytes):
    return pltpu.CompilerParams(vmem_limit_bytes=mebibytes << 20)


def swap_route(count, bit):
    return [(low, low ^ (1 << bit)) for low in range(count) if low ^ (1 << bit) < count]


def dot(a, b, dims):
    return lax.dot_general(a, b, (dims, ((), ())), preferred_element_type=F32)


def halves(value):
    high = value.astype(BF16)
    return high, (value - high.astype(F32)).astype(BF16)


def grams_of(slots, order, fbuf, cbuf):
    products = [dot(fbuf[i], cbuf[i], ((1,), (0,))) for i in range(len(slots))]
    operators = []
    for slot, product in zip(slots, products):
        width = product.shape[0] * (2 + order[slot]) // 4
        keep = lax.broadcasted_iota(I32, product.shape, 0) < width
        operators.append(jnp.where(keep, product, 0.0).astype(BF16))
    return [dot(operator, operator, ((0,), (0,))) for operator in operators]


def one_hot(index, rows):
    hit = lax.broadcasted_iota(I32, (rows, index.shape[1]), 0) == index
    return jnp.where(hit, 1.0, 0.0).astype(BF16)


def parities():
    return lax.axis_index("gx") % 2, lax.axis_index("gz") % 2


def cell_of(cell, fx, fz):
    odd_x, odd_z = parities()
    pitch = fz + 2
    row = jnp.zeros_like(cell)
    for edge in range(1, fx + 2):
        row = row + jnp.where(cell >= edge * pitch, 1, 0)
    column = cell - row * pitch
    base_x = fx * fz
    base_z = base_x + 2 * fz
    out = (row - 1) * fz + column - 1
    out = jnp.where(column == fz + 1, base_z + odd_z * fx + row - 1, out)
    out = jnp.where(column == 0, base_z + (1 - odd_z) * fx + row - 1, out)
    out = jnp.where(row == fx + 1, base_x + odd_x * fz + column - 1, out)
    return jnp.where(row == 0, base_x + (1 - odd_x) * fz + column - 1, out)


def edges_of(field, fx, fz):
    odd_x, odd_z = parities()
    own = fx * fz
    last, first = field[own - fz :, :], field[:fz, :]
    row = lax.broadcasted_iota(I32, (2 * fx, own), 0)
    wanted = jnp.where(row < fx, row * fz + fz - 1, (row - fx) * fz)
    hit = lax.broadcasted_iota(I32, (2 * fx, own), 1) == wanted
    sides = dot(jnp.where(hit, 1.0, 0.0).astype(BF16), field, ((1,), (0,)))
    right, left = sides[:fx], sides[fx:]
    flip_x, flip_z = odd_x == 1, odd_z == 1
    return (
        jnp.where(flip_x, first, last),
        jnp.where(flip_x, last, first),
        jnp.where(flip_z, left, right).astype(BF16),
        jnp.where(flip_z, right, left).astype(BF16),
    )


def started(*copies):
    for copy in copies:
        copy.start()
    return copies


def waited(copies):
    for copy in copies:
        copy.wait()


def fetch(slots, factor, coupling, fbuf, cbuf, sem):
    copies = []
    for i, slot in enumerate(slots):
        copies += started(
            pltpu.make_async_copy(factor.at[slot], fbuf.at[i], sem.at[i, 0]),
            pltpu.make_async_copy(coupling.at[slot], cbuf.at[i], sem.at[i, 1]),
        )
    return copies


def given_kernel(
    fx, fz, f_hbm, order_hbm, factor, coupling, traces_hbm, out, e0, e1, e3,
    f, order, traces, fbuf, cbuf, sem, small,
):
    moves = f.shape[0]
    unknowns = coupling.shape[2]
    index, rest, block = started(
        pltpu.make_async_copy(f_hbm, f, small.at[0]),
        pltpu.make_async_copy(order_hbm, order, small.at[1]),
        pltpu.make_async_copy(traces_hbm, traces, small.at[2]),
    )
    index.wait()
    slots = [f[i] for i in range(moves)]
    copies = fetch(slots, factor, coupling, fbuf, cbuf, sem)
    block.wait()
    e0[...], e1[...], side, e3[...] = edges_of(traces[...], fx, fz)
    for i in range(side.shape[1] // unknowns):
        part = side[:, i * unknowns : (i + 1) * unknowns]
        out[pl.ds(moves * unknowns + i * fx, fx), :] = part
    rest.wait()
    waited(copies)
    for i, gram in enumerate(grams_of(slots, order, fbuf, cbuf)):
        out[pl.ds(i * unknowns, unknowns), :] = gram.astype(BF16)


def kept_kernel(
    fx, fz, f, s, order, reads, writes, factor, coupling, given, part, moved_to, moved_from,
    fbuf, cbuf, to, origin, kept, sem,
):
    slots, moves = reads.shape[0], f.shape[0]
    unknowns = reads.shape[1]
    most = slots - moves
    own, cells = fx * fz, origin.shape[0]
    for i in range(slots):
        kept[i] = 0
    count = jnp.int32(0)
    for slot in range(slots):
        moved = f[0] == slot
        for i in range(moves):
            moved = moved | (f[i] == slot) | (s[i] == slot)
        kept[count] = slot
        count = count + jnp.where(moved, 0, 1)
    wanted = [s[i] for i in range(moves)] + [kept[i] for i in range(most)]
    copies = fetch(wanted, factor, coupling, fbuf, cbuf, sem)

    def place(slot, valid, to_ref, from_ref, i):
        read = jnp.where(valid, cell_of(reads[pl.ds(slot, 1), :], fx, fz), -1)
        write = jnp.where(valid, writes[pl.ds(slot, 1), :], -1)
        columns = pl.ds(i * unknowns, unknowns)
        to_ref[:, columns] = one_hot(write, own)
        from_ref[:, columns] = one_hot(read, cells)

    for i in range(moves):
        place(s[i], True, moved_to, moved_from, i)
        stays = f[i] != s[0]
        for j in range(1, moves):
            stays = stays & (f[i] != s[j])
        place(f[i], stays, moved_to, moved_from, moves + i)
    for i in range(most):
        place(kept[i], i < count, to, origin, i)

    waited(copies)
    grams = grams_of(wanted, order, fbuf, cbuf)
    for i in range(moves):
        given[pl.ds(i * unknowns, unknowns), :] = grams[i].astype(BF16)
    highs, lows = [], []
    for i in range(most):
        scatter = to[:, pl.ds(i * unknowns, unknowns)]
        gram = jnp.concatenate(halves(grams[moves + i]), axis=0)
        spread = dot(jnp.concatenate([scatter, scatter], axis=1), gram, ((1,), (0,)))
        high, low = halves(spread)
        highs.append(high)
        lows.append(low)
    left = jnp.concatenate(
        [jnp.concatenate(highs, axis=1), jnp.concatenate(lows, axis=1)], axis=0
    )
    both = dot(left, origin[...], ((1,), (1,)))
    part[...] = both[:own] + both[own:]


def relay_kernel(f, s, given, got, out):
    moves = f.shape[0]
    unknowns = given.shape[0] // moves
    for i in range(moves):
        value = given[pl.ds(i * unknowns, unknowns), :]
        for j in range(moves):
            value = jnp.where(s[i] == f[j], got[pl.ds(j * unknowns, unknowns), :], value)
        out[pl.ds(i * unknowns, unknowns), :] = value


def applied(matrix, field, frame):
    both = dot(matrix, jnp.concatenate([field, frame], axis=0), ((1,), (0,)))
    own = matrix.shape[0] // 2
    return both[:own] + both[own:]


def first_kernel(
    fx, fz, moves, got, got_s, part, moved_to, moved_from, traces, h0, h1, h3,
    matrix, first, e0, e1, e2, e3,
):
    columns = traces.shape[1]
    unknowns = got.shape[1]
    spread = []
    for i in range(2 * moves):
        source = got_s if i < moves else got
        gram = source[pl.ds(i % moves * unknowns, unknowns), :]
        scatter = moved_to[:, pl.ds(i * unknowns, unknowns)]
        spread.append(dot(scatter, gram, ((1,), (0,))).astype(BF16))
    moved = dot(jnp.concatenate(spread, axis=1), moved_from[...], ((1,), (1,)))
    whole = jnp.concatenate(halves(part[...] + moved), axis=0)
    matrix[...] = whole
    side = [
        got[pl.ds(moves * unknowns + i * fx, fx), :] for i in range(columns // unknowns)
    ]
    side = jnp.concatenate(side, axis=1)
    frame = jnp.concatenate([h0[...], h1[...], side, h3[...]], axis=0)
    field = applied(whole, traces[...], frame).astype(BF16)
    first[...] = field
    e0[...], e1[...], e2[...], e3[...] = edges_of(field, fx, fz)


def second_kernel(matrix, first, h0, h1, h2, h3, out):
    frame = jnp.concatenate([h0[...], h1[...], h2[...], h3[...]], axis=0)
    out[...] = applied(matrix[...], first[...], frame)


def pairs(count, odd):
    route = []
    for low in range(odd, count - 1, 2):
        route += [(low, low + 1), (low + 1, low)]
    return route


def swapped(edge, axis, odd):
    return lax.ppermute(edge, axis, pairs(lax.axis_size(axis), odd))


def body(
    gram_factor, coupling, order_class, first_moves, second_moves, trace_index, owner_index, traces
):
    slots, width, unknowns = coupling.shape
    moves = first_moves.shape[0]
    fx, _, fz, columns = traces.shape
    own = fx * fz
    cells = own + 2 * (fx + fz)
    most = slots - moves
    field = traces.reshape(own, columns)
    grams = jax.ShapeDtypeStruct((moves * unknowns, unknowns), BF16)
    load = jax.ShapeDtypeStruct((moves * unknowns + fx * columns // unknowns, unknowns), BF16)
    edges = [jax.ShapeDtypeStruct((n, columns), BF16) for n in (fz, fz, fx, fx)]

    def in_hbm(array):
        return pltpu.with_memory_space_constraint(array, pltpu.MemorySpace.HBM)

    gram_factor, coupling = in_hbm(gram_factor), in_hbm(coupling)

    def element_cost(count):
        return pl.CostEstimate(
            flops=2 * count * width * unknowns * (width + unknowns),
            bytes_accessed=2 * count * width * (width + unknowns),
            transcendentals=0,
        )

    def buffers(count):
        return [
            pltpu.VMEM((count, width, width), BF16),
            pltpu.VMEM((count, width, unknowns), BF16),
        ]

    given, t0, t1, t3 = pl.pallas_call(
        functools.partial(given_kernel, fx, fz),
        out_shape=(load, edges[0], edges[1], edges[3]),
        in_specs=[HBM] * 5,
        out_specs=(VMEM,) * 4,
        scratch_shapes=[
            pltpu.SMEM((moves,), I32),
            pltpu.SMEM((slots,), I32),
            pltpu.VMEM((own, columns), BF16),
            *buffers(moves),
            pltpu.SemaphoreType.DMA((moves, 2)),
            pltpu.SemaphoreType.DMA((3,)),
        ],
        compiler_params=params(12),
        cost_estimate=element_cost(moves),
        name="given",
    )(in_hbm(first_moves), in_hbm(order_class), gram_factor, coupling, in_hbm(field))
    given, t0, t1, t3, second_moves = lax.optimization_barrier((given, t0, t1, t3, second_moves))
    got = swapped(given, "gz", 0)

    given_s, part, moved_to, moved_from = pl.pallas_call(
        functools.partial(kept_kernel, fx, fz),
        out_shape=(
            grams,
            jax.ShapeDtypeStruct((own, cells), F32),
            jax.ShapeDtypeStruct((own, 2 * moves * unknowns), BF16),
            jax.ShapeDtypeStruct((cells, 2 * moves * unknowns), BF16),
        ),
        in_specs=[SMEM] * 3 + [VMEM] * 2 + [HBM] * 2,
        out_specs=(VMEM,) * 4,
        scratch_shapes=[
            *buffers(slots),
            pltpu.VMEM((own, most * unknowns), BF16),
            pltpu.VMEM((cells, most * unknowns), BF16),
            pltpu.SMEM((slots,), I32),
            pltpu.SemaphoreType.DMA((slots, 2)),
        ],
        compiler_params=params(24),
        cost_estimate=element_cost(slots),
        name="kept",
    )(
        first_moves, second_moves, order_class, trace_index, owner_index, gram_factor, coupling
    )

    relayed = pl.pallas_call(
        relay_kernel,
        out_shape=grams,
        in_specs=[SMEM] * 2 + [VMEM] * 2,
        out_specs=VMEM,
        compiler_params=params(2),
        name="relay",
    )(first_moves, second_moves, given_s, got)
    both = lax.axis_size("gy") * lax.axis_size("gz")
    second_bit = lax.axis_size("gz").bit_length() - 1
    got_s = lax.ppermute(relayed, ("gy", "gz"), swap_route(both, second_bit))
    h1 = swapped(t1, "gx", 1)
    h3 = swapped(t3, "gz", 1)
    h0 = swapped(t0, "gx", 0)

    matrix, first, *first_edges = pl.pallas_call(
        functools.partial(first_kernel, fx, fz, moves),
        out_shape=(
            jax.ShapeDtypeStruct((2 * own, cells), BF16),
            jax.ShapeDtypeStruct((own, columns), BF16),
            *edges,
        ),
        in_specs=[VMEM] * 9,
        out_specs=(VMEM,) * 6,
        compiler_params=params(12),
        name="first",
    )(got, got_s, part, moved_to, moved_from, field, h0, h1, h3)

    e0, e1, e2, e3 = first_edges
    h1 = swapped(e1, "gx", 1)
    h2 = swapped(e2, "gz", 0)
    h3 = swapped(e3, "gz", 1)
    h0 = swapped(e0, "gx", 0)
    second = pl.pallas_call(
        second_kernel,
        out_shape=jax.ShapeDtypeStruct((own, columns), F32),
        in_specs=[VMEM] * 6,
        out_specs=VMEM,
        compiler_params=params(6),
        name="second",
    )(matrix, first, h0, h1, h2, h3)
    return second.reshape(traces.shape)


def solution(mesh):
    return jax.shard_map(
        body,
        mesh=mesh,
        in_specs=(
            P(("gx", "gy", "gz"), None, None),
            P(("gx", "gy", "gz"), None, None),
            P(("gx", "gy", "gz")),
            P(("gx", "gy", "gz")),
            P(("gx", "gy", "gz")),
            P(("gx", "gy", "gz"), None),
            P(("gx", "gy", "gz"), None),
            P("gx", "gy", "gz", None),
        ),
        out_specs=P("gx", "gy", "gz", None),
        check_vma=False,
    )
```

```python
import functools

import jax
import jax.numpy as jnp
from jax import lax
from jax.experimental import pallas as pl
from jax.experimental.pallas import tpu as pltpu
from jax.sharding import PartitionSpec as P

BF16 = jnp.bfloat16
F32 = jnp.float32
I32 = jnp.int32
HBM = pl.BlockSpec(memory_space=pltpu.MemorySpace.HBM)
VMEM = pl.BlockSpec(memory_space=pltpu.MemorySpace.VMEM)
SMEM = pl.BlockSpec(memory_space=pltpu.MemorySpace.SMEM)


def params(mebibytes):
    return pltpu.CompilerParams(vmem_limit_bytes=int(mebibytes * 1048576))


def swap_route(count, bit):
    return [(low, low ^ (1 << bit)) for low in range(count) if low ^ (1 << bit) < count]


def dot(a, b, dims):
    return lax.dot_general(a, b, (dims, ((), ())), preferred_element_type=F32)


def halves(value):
    high = value.astype(BF16)
    return high, (value - high.astype(F32)).astype(BF16)


def grams_of(slots, order, fbuf, cbuf):
    products = [dot(fbuf[i], cbuf[i], ((1,), (0,))).astype(BF16) for i in range(len(slots))]
    operators = []
    for slot, product in zip(slots, products):
        rows = product.shape[0]
        bounds = [rows * (2 + c) // 4 for c in range(3)]
        parts = [product[: bounds[0]]]
        for c in (1, 2):
            part = product[bounds[c - 1] : bounds[c]]
            parts.append(jnp.where(order[slot] >= c, part, jnp.zeros_like(part)))
        operators.append(jnp.concatenate(parts, axis=0))
    return [dot(operator, operator, ((0,), (0,))) for operator in operators]


def one_hot(index, rows):
    tile = 16
    shape = (tile, index.shape[1])
    here = lax.broadcasted_iota(I32, shape, 0) == (index & (tile - 1))
    block = jnp.where(here, index >> 4, -1).astype(F32).astype(BF16)
    one, zero = jnp.ones(shape, BF16), jnp.zeros(shape, BF16)
    return jnp.concatenate(
        [jnp.where(block == jnp.full(shape, i, BF16), one, zero) for i in range(rows // tile)],
        axis=0,
    )


def parities():
    return lax.axis_index("gx") % 2, lax.axis_index("gz") % 2


def cell_of(cell, fx, fz):
    odd_x, odd_z = parities()
    pitch = fz + 2
    row = jnp.zeros_like(cell)
    for edge in range(1, fx + 2):
        row = row + jnp.where(cell >= edge * pitch, 1, 0)
    column = cell - row * pitch
    base_x = fx * fz
    base_z = base_x + 2 * fz
    out = (row - 1) * fz + column - 1
    out = jnp.where(column == fz + 1, base_z + odd_z * fx + row - 1, out)
    out = jnp.where(column == 0, base_z + (1 - odd_z) * fx + row - 1, out)
    out = jnp.where(row == fx + 1, base_x + odd_x * fz + column - 1, out)
    return jnp.where(row == 0, base_x + (1 - odd_x) * fz + column - 1, out)


def edges_of(field, fx, fz):
    odd_x, odd_z = parities()
    own = fx * fz
    last, first = field[own - fz :, :], field[:fz, :]
    row = lax.broadcasted_iota(I32, (2 * fx, own), 0)
    wanted = jnp.where(row < fx, row * fz + fz - 1, (row - fx) * fz)
    hit = lax.broadcasted_iota(I32, (2 * fx, own), 1) == wanted
    sides = dot(jnp.where(hit, 1.0, 0.0).astype(BF16), field, ((1,), (0,)))
    right, left = sides[:fx], sides[fx:]
    flip_x, flip_z = odd_x == 1, odd_z == 1
    return (
        jnp.where(flip_x, first, last),
        jnp.where(flip_x, last, first),
        jnp.where(flip_z, left, right).astype(BF16),
        jnp.where(flip_z, right, left).astype(BF16),
    )


def started(*copies):
    for copy in copies:
        copy.start()
    return copies


def waited(copies):
    for copy in copies:
        copy.wait()


def fetch(slots, factor, coupling, fbuf, cbuf, sem):
    copies = []
    for i, slot in enumerate(slots):
        copies += started(
            pltpu.make_async_copy(factor.at[slot], fbuf.at[i], sem.at[i, 0]),
            pltpu.make_async_copy(coupling.at[slot], cbuf.at[i], sem.at[i, 1]),
        )
    return copies


def given_kernel(
    fx, fz, f_hbm, order_hbm, factor, coupling, traces_hbm, out, e0, e1, e3,
    f, order, traces, fbuf, cbuf, sem, small,
):
    moves = f.shape[0]
    unknowns = coupling.shape[2]
    index, rest, block = started(
        pltpu.make_async_copy(f_hbm, f, small.at[0]),
        pltpu.make_async_copy(order_hbm, order, small.at[1]),
        pltpu.make_async_copy(traces_hbm, traces, small.at[2]),
    )
    index.wait()
    slots = [f[i] for i in range(moves)]
    copies = fetch(slots, factor, coupling, fbuf, cbuf, sem)
    block.wait()
    e0[...], e1[...], side, e3[...] = edges_of(traces[...], fx, fz)
    for i in range(side.shape[1] // unknowns):
        part = side[:, i * unknowns : (i + 1) * unknowns]
        out[pl.ds(moves * unknowns + i * fx, fx), :] = part
    rest.wait()
    waited(copies)
    for i, gram in enumerate(grams_of(slots, order, fbuf, cbuf)):
        out[pl.ds(i * unknowns, unknowns), :] = gram.astype(BF16)


def kept_kernel(
    fx, fz, f, s, order, reads, writes, factor, coupling,
    given, part, moved_to, moved_from, relayed,
    to, origin, left, grams, places, rest,
):
    slots, moves = reads.shape[0], f.shape[0]
    unknowns = reads.shape[1]
    most = slots - moves
    own, cells = fx * fz, origin.shape[0]

    def among(slot, moved):
        found = moved[0] == slot
        for j in range(1, moves):
            found = found | (moved[j] == slot)
        return found

    count = jnp.int32(0)
    for slot in range(slots):
        rest[count] = slot
        count = count + jnp.where(among(slot, f), 0, 1)
    wanted = [rest[i] for i in range(most)]
    places[...] = cell_of(reads[...], fx, fz)

    def place(slot, valid, to_ref, from_ref, i):
        read = jnp.where(valid, places[pl.ds(slot, 1), :], -1)
        write = jnp.where(valid, writes[pl.ds(slot, 1), :], -1)
        columns = pl.ds(i * unknowns, unknowns)
        to_ref[:, columns] = one_hot(write, own)
        from_ref[:, columns] = one_hot(read, cells)

    tile = (16, unknowns)
    for i in range(moves):
        place(s[i], True, moved_to, moved_from, i)
        place(f[i], jnp.logical_not(among(f[i], s)), moved_to, moved_from, moves + i)
        for j in range(moves):
            same = jnp.where(s[i] == f[j], 1.0, 0.0)
            relayed[pl.ds((i * moves + j) * 16, 16), :] = jnp.full(tile, same, F32).astype(BF16)
    for i, slot in enumerate(wanted):
        place(slot, jnp.logical_not(among(slot, s)), to, origin, i)

    factors, couplings = [factor[slot] for slot in wanted], [coupling[slot] for slot in wanted]
    for i, exact in enumerate(grams_of(wanted, order, factors, couplings)):
        columns = pl.ds(i * unknowns, unknowns)
        high, low = halves(exact)
        grams[columns, :] = high
        scatter = to[:, columns]
        spread = dot(
            jnp.concatenate([scatter, scatter], axis=1),
            jnp.concatenate([high, low], axis=0),
            ((1,), (0,)),
        )
        high, low = halves(spread)
        left[:own, columns] = high
        left[own:, columns] = low
    both = dot(left[...], origin[...], ((1,), (1,)))
    part[...] = both[:own] + both[own:]
    for i in range(moves):
        at = s[i]
        for j in range(moves):
            at = at - jnp.where(f[j] < s[i], 1, 0)
        at = jnp.minimum(at, most - 1)
        source = pl.ds(pl.multiple_of(at * unknowns, unknowns), unknowns)
        given[pl.ds(i * unknowns, unknowns), :] = grams[source, :]


def relay_kernel(moves, relayed, given, got, out):
    unknowns = given.shape[0] // moves
    for i in range(moves):
        value = given[pl.ds(i * unknowns, unknowns), :]
        for j in range(moves):
            same = relayed[pl.ds((i * moves + j) * 16, 16), :]
            same = jnp.concatenate([same] * (unknowns // 16), axis=0)
            value = jnp.where(
                same > jnp.zeros_like(same), got[pl.ds(j * unknowns, unknowns), :], value
            )
        out[pl.ds(i * unknowns, unknowns), :] = value


def applied(matrix, field, frame):
    both = dot(matrix, jnp.concatenate([field, frame], axis=0), ((1,), (0,)))
    own = matrix.shape[0] // 2
    return both[:own] + both[own:]


def first_kernel(
    fx, fz, moves, got, got_s, part, moved_to, moved_from, traces, h0, h1, h3,
    matrix, first, e0, e1, e2, e3,
):
    columns = traces.shape[1]
    unknowns = got.shape[1]
    spread = []
    for i in range(2 * moves):
        source = got_s if i < moves else got
        gram = source[pl.ds(i % moves * unknowns, unknowns), :]
        scatter = moved_to[:, pl.ds(i * unknowns, unknowns)]
        spread.append(dot(scatter, gram, ((1,), (0,))).astype(BF16))
    moved = dot(jnp.concatenate(spread, axis=1), moved_from[...], ((1,), (1,)))
    whole = jnp.concatenate(halves(part[...] + moved), axis=0)
    matrix[...] = whole
    side = [
        got[pl.ds(moves * unknowns + i * fx, fx), :] for i in range(columns // unknowns)
    ]
    side = jnp.concatenate(side, axis=1)
    frame = jnp.concatenate([h0[...], h1[...], side, h3[...]], axis=0)
    field = applied(whole, traces[...], frame).astype(BF16)
    first[...] = field
    e0[...], e1[...], e2[...], e3[...] = edges_of(field, fx, fz)


def second_kernel(matrix, first, h0, h1, h2, h3, out):
    frame = jnp.concatenate([h0[...], h1[...], h2[...], h3[...]], axis=0)
    out[...] = applied(matrix[...], first[...], frame)


def pairs(count, odd):
    route = []
    for low in range(odd, count - 1, 2):
        route += [(low, low + 1), (low + 1, low)]
    return route


def swapped(edge, axis, odd):
    return lax.ppermute(edge, axis, pairs(lax.axis_size(axis), odd))


def body(
    gram_factor, coupling, order_class, first_moves, second_moves, trace_index, owner_index, traces
):
    slots, width, unknowns = coupling.shape
    moves = first_moves.shape[0]
    fx, _, fz, columns = traces.shape
    own = fx * fz
    cells = own + 2 * (fx + fz)
    most = slots - moves
    field = traces.reshape(own, columns)
    grams = jax.ShapeDtypeStruct((moves * unknowns, unknowns), BF16)
    load = jax.ShapeDtypeStruct((moves * unknowns + fx * columns // unknowns, unknowns), BF16)
    edges = [jax.ShapeDtypeStruct((n, columns), BF16) for n in (fz, fz, fx, fx)]

    def in_hbm(array):
        return pltpu.with_memory_space_constraint(array, pltpu.MemorySpace.HBM)


    def element_cost(count):
        return pl.CostEstimate(
            flops=2 * count * width * unknowns * (width + unknowns),
            bytes_accessed=2 * count * width * (width + unknowns),
            transcendentals=0,
        )

    def buffers(count):
        return [
            pltpu.VMEM((count, width, width), BF16),
            pltpu.VMEM((count, width, unknowns), BF16),
        ]

    given, t0, t1, t3 = pl.pallas_call(
        functools.partial(given_kernel, fx, fz),
        out_shape=(load, edges[0], edges[1], edges[3]),
        in_specs=[HBM] * 5,
        out_specs=(VMEM,) * 4,
        scratch_shapes=[
            pltpu.SMEM((moves,), I32),
            pltpu.SMEM((slots,), I32),
            pltpu.VMEM((own, columns), BF16),
            *buffers(moves),
            pltpu.SemaphoreType.DMA((moves, 2)),
            pltpu.SemaphoreType.DMA((3,)),
        ],
        compiler_params=params(53),
        cost_estimate=element_cost(moves),
        name="given",
    )(
        in_hbm(first_moves), in_hbm(order_class), in_hbm(gram_factor), in_hbm(coupling),
        in_hbm(field),
    )
    given, t0, t1, t3, gram_factor, coupling = lax.optimization_barrier(
        (given, t0, t1, t3, gram_factor, coupling)
    )
    got = swapped(given, "gz", 0)

    given_s, part, moved_to, moved_from, same = pl.pallas_call(
        functools.partial(kept_kernel, fx, fz),
        out_shape=(
            grams,
            jax.ShapeDtypeStruct((own, cells), F32),
            jax.ShapeDtypeStruct((own, 2 * moves * unknowns), BF16),
            jax.ShapeDtypeStruct((cells, 2 * moves * unknowns), BF16),
            jax.ShapeDtypeStruct((16 * moves * moves, unknowns), BF16),
        ),
        in_specs=[SMEM] * 3 + [VMEM] * 4,
        out_specs=(VMEM,) * 5,
        scratch_shapes=[
            pltpu.VMEM((own, most * unknowns), BF16),
            pltpu.VMEM((cells, most * unknowns), BF16),
            pltpu.VMEM((2 * own, most * unknowns), BF16),
            pltpu.VMEM((most * unknowns, unknowns), BF16),
            pltpu.VMEM((slots, unknowns), I32),
            pltpu.SMEM((slots,), I32),
        ],
        compiler_params=params(24),
        cost_estimate=element_cost(most),
        name="kept",
    )(
        first_moves, second_moves, order_class, trace_index, owner_index, gram_factor, coupling
    )

    relayed = pl.pallas_call(
        functools.partial(relay_kernel, moves),
        out_shape=grams,
        in_specs=[VMEM] * 3,
        out_specs=VMEM,
        compiler_params=params(2),
        name="relay",
    )(same, given_s, got)
    both = lax.axis_size("gy") * lax.axis_size("gz")
    second_bit = lax.axis_size("gz").bit_length() - 1
    got_s = lax.ppermute(relayed, ("gy", "gz"), swap_route(both, second_bit))
    h1 = swapped(t1, "gx", 1)
    h3 = swapped(t3, "gz", 1)
    h0 = swapped(t0, "gx", 0)

    matrix, first, *first_edges = pl.pallas_call(
        functools.partial(first_kernel, fx, fz, moves),
        out_shape=(
            jax.ShapeDtypeStruct((2 * own, cells), BF16),
            jax.ShapeDtypeStruct((own, columns), BF16),
            *edges,
        ),
        in_specs=[VMEM] * 9,
        out_specs=(VMEM,) * 6,
        compiler_params=params(12),
        name="first",
    )(got, got_s, part, moved_to, moved_from, field, h0, h1, h3)

    e0, e1, e2, e3 = first_edges
    h1 = swapped(e1, "gx", 1)
    h2 = swapped(e2, "gz", 0)
    h3 = swapped(e3, "gz", 1)
    h0 = swapped(e0, "gx", 0)
    second = pl.pallas_call(
        second_kernel,
        out_shape=jax.ShapeDtypeStruct((own, columns), F32),
        in_specs=[VMEM] * 6,
        out_specs=VMEM,
        compiler_params=params(6),
        name="second",
    )(matrix, first, h0, h1, h2, h3)
    return second.reshape(traces.shape)


def solution(mesh):
    return jax.shard_map(
        body,
        mesh=mesh,
        in_specs=(
            P(("gx", "gy", "gz"), None, None),
            P(("gx", "gy", "gz"), None, None),
            P(("gx", "gy", "gz")),
            P(("gx", "gy", "gz")),
            P(("gx", "gy", "gz")),
            P(("gx", "gy", "gz"), None),
            P(("gx", "gy", "gz"), None),
            P("gx", "gy", "gz", None),
        ),
        out_specs=P("gx", "gy", "gz", None),
        check_vma=False,
    )
```

```python
import functools

import jax
import jax.numpy as jnp
from jax import lax
from jax.experimental import pallas as pl
from jax.experimental.pallas import tpu as pltpu
from jax.sharding import PartitionSpec as P

BF16 = jnp.bfloat16
F32 = jnp.float32
I32 = jnp.int32
HBM = pl.BlockSpec(memory_space=pltpu.MemorySpace.HBM)
VMEM = pl.BlockSpec(memory_space=pltpu.MemorySpace.VMEM)
SMEM = pl.BlockSpec(memory_space=pltpu.MemorySpace.SMEM)


def params(mebibytes):
    return pltpu.CompilerParams(vmem_limit_bytes=int(mebibytes * 1048576))


def swap_route(count, bit):
    return [(low, low ^ (1 << bit)) for low in range(count) if low ^ (1 << bit) < count]


def dot(a, b, dims):
    return lax.dot_general(a, b, (dims, ((), ())), preferred_element_type=F32)


def halves(value):
    high = value.astype(BF16)
    return high, (value - high.astype(F32)).astype(BF16)


def grams_of(slots, order, fbuf, cbuf):
    products = [dot(fbuf[i], cbuf[i], ((1,), (0,))).astype(BF16) for i in range(len(slots))]
    operators = []
    for slot, product in zip(slots, products):
        rows = product.shape[0]
        bounds = [rows * (2 + c) // 4 for c in range(3)]
        parts = [product[: bounds[0]]]
        for c in (1, 2):
            part = product[bounds[c - 1] : bounds[c]]
            parts.append(jnp.where(order[slot] >= c, part, jnp.zeros_like(part)))
        operators.append(jnp.concatenate(parts, axis=0))
    return [dot(operator, operator, ((0,), (0,))) for operator in operators]


def one_hot(index, rows):
    tile = 16
    shape = (tile, index.shape[1])
    here = lax.broadcasted_iota(I32, shape, 0) == (index & (tile - 1))
    block = jnp.where(here, index >> 4, -1).astype(F32).astype(BF16)
    one, zero = jnp.ones(shape, BF16), jnp.zeros(shape, BF16)
    return jnp.concatenate(
        [jnp.where(block == jnp.full(shape, i, BF16), one, zero) for i in range(rows // tile)],
        axis=0,
    )


def parities():
    return lax.axis_index("gx") % 2, lax.axis_index("gz") % 2


def cell_of(cell, fx, fz):
    odd_x, odd_z = parities()
    pitch = fz + 2
    row = jnp.zeros_like(cell)
    for edge in range(1, fx + 2):
        row = row + jnp.where(cell >= edge * pitch, 1, 0)
    column = cell - row * pitch
    base_x = fx * fz
    base_z = base_x + 2 * fz
    out = (row - 1) * fz + column - 1
    out = jnp.where(column == fz + 1, base_z + odd_z * fx + row - 1, out)
    out = jnp.where(column == 0, base_z + (1 - odd_z) * fx + row - 1, out)
    out = jnp.where(row == fx + 1, base_x + odd_x * fz + column - 1, out)
    return jnp.where(row == 0, base_x + (1 - odd_x) * fz + column - 1, out)


def edges_of(field, fx, fz):
    odd_x, odd_z = parities()
    own = fx * fz
    last, first = field[own - fz :, :], field[:fz, :]
    row = lax.broadcasted_iota(I32, (2 * fx, own), 0)
    wanted = jnp.where(row < fx, row * fz + fz - 1, (row - fx) * fz)
    hit = lax.broadcasted_iota(I32, (2 * fx, own), 1) == wanted
    sides = dot(jnp.where(hit, 1.0, 0.0).astype(BF16), field, ((1,), (0,)))
    right, left = sides[:fx], sides[fx:]
    flip_x, flip_z = odd_x == 1, odd_z == 1
    return (
        jnp.where(flip_x, first, last),
        jnp.where(flip_x, last, first),
        jnp.where(flip_z, left, right).astype(BF16),
        jnp.where(flip_z, right, left).astype(BF16),
    )


def started(*copies):
    for copy in copies:
        copy.start()
    return copies


def waited(copies):
    for copy in copies:
        copy.wait()


def fetch(slots, factor, coupling, fbuf, cbuf, sem):
    copies = []
    for i, slot in enumerate(slots):
        copies += started(
            pltpu.make_async_copy(factor.at[slot], fbuf.at[i], sem.at[i, 0]),
            pltpu.make_async_copy(coupling.at[slot], cbuf.at[i], sem.at[i, 1]),
        )
    return copies


def given_kernel(
    fx, fz, f_hbm, order_hbm, factor, coupling, traces_hbm, out, e0, e1, e3,
    f, order, traces, fbuf, cbuf, sem, small,
):
    moves = f.shape[0]
    unknowns = coupling.shape[2]
    index, rest, block = started(
        pltpu.make_async_copy(f_hbm, f, small.at[0]),
        pltpu.make_async_copy(order_hbm, order, small.at[1]),
        pltpu.make_async_copy(traces_hbm, traces, small.at[2]),
    )
    index.wait()
    slots = [f[i] for i in range(moves)]
    copies = fetch(slots, factor, coupling, fbuf, cbuf, sem)
    block.wait()
    e0[...], e1[...], side, e3[...] = edges_of(traces[...], fx, fz)
    for i in range(side.shape[1] // unknowns):
        part = side[:, i * unknowns : (i + 1) * unknowns]
        out[pl.ds(moves * unknowns + i * fx, fx), :] = part
    rest.wait()
    waited(copies)
    for i, gram in enumerate(grams_of(slots, order, fbuf, cbuf)):
        out[pl.ds(i * unknowns, unknowns), :] = gram.astype(BF16)


def kept_kernel(
    fx, fz, f, s, order, reads, writes, factor, coupling,
    given, part, moved_to, moved_from, relayed,
    to, origin, left, grams, places, rest,
):
    slots, moves = reads.shape[0], f.shape[0]
    unknowns = reads.shape[1]
    most = slots - moves
    own, cells = fx * fz, origin.shape[0]

    def among(slot, moved):
        found = moved[0] == slot
        for j in range(1, moves):
            found = found | (moved[j] == slot)
        return found

    count = jnp.int32(0)
    for slot in range(slots):
        rest[count] = slot
        count = count + jnp.where(among(slot, f), 0, 1)
    wanted = [rest[i] for i in range(most)]
    places[...] = cell_of(reads[...], fx, fz)

    def place(slot, valid, to_ref, from_ref, i):
        read = jnp.where(valid, places[pl.ds(slot, 1), :], -1)
        write = jnp.where(valid, writes[pl.ds(slot, 1), :], -1)
        columns = pl.ds(i * unknowns, unknowns)
        to_ref[:, columns] = one_hot(write, own)
        from_ref[:, columns] = one_hot(read, cells)

    tile = (16, unknowns)
    for i in range(moves):
        place(s[i], True, moved_to, moved_from, i)
        place(f[i], jnp.logical_not(among(f[i], s)), moved_to, moved_from, moves + i)
        for j in range(moves):
            same = jnp.where(s[i] == f[j], 1.0, 0.0)
            relayed[pl.ds((i * moves + j) * 16, 16), :] = jnp.full(tile, same, F32).astype(BF16)
    for i, slot in enumerate(wanted):
        place(slot, jnp.logical_not(among(slot, s)), to, origin, i)

    factors, couplings = [factor[slot] for slot in wanted], [coupling[slot] for slot in wanted]
    for i, exact in enumerate(grams_of(wanted, order, factors, couplings)):
        columns = pl.ds(i * unknowns, unknowns)
        high, low = halves(exact)
        grams[columns, :] = high
        scatter = to[:, columns]
        spread = dot(
            jnp.concatenate([scatter, scatter], axis=1),
            jnp.concatenate([high, low], axis=0),
            ((1,), (0,)),
        )
        high, low = halves(spread)
        left[:own, columns] = high
        left[own:, columns] = low
    both = dot(left[...], origin[...], ((1,), (1,)))
    part[...] = both[:own] + both[own:]
    for i in range(moves):
        at = s[i]
        for j in range(moves):
            at = at - jnp.where(f[j] < s[i], 1, 0)
        at = jnp.minimum(at, most - 1)
        source = pl.ds(pl.multiple_of(at * unknowns, unknowns), unknowns)
        given[pl.ds(i * unknowns, unknowns), :] = grams[source, :]


def relay_kernel(moves, relayed, given, got, out):
    unknowns = given.shape[0] // moves
    for i in range(moves):
        value = given[pl.ds(i * unknowns, unknowns), :]
        for j in range(moves):
            same = relayed[pl.ds((i * moves + j) * 16, 16), :]
            same = jnp.concatenate([same] * (unknowns // 16), axis=0)
            value = jnp.where(
                same > jnp.zeros_like(same), got[pl.ds(j * unknowns, unknowns), :], value
            )
        out[pl.ds(i * unknowns, unknowns), :] = value


def applied(matrix, field, frame):
    both = dot(matrix, jnp.concatenate([field, frame], axis=0), ((1,), (0,)))
    own = matrix.shape[0] // 2
    return both[:own] + both[own:]


def first_kernel(
    fx, fz, moves, got, got_s, part, moved_to, moved_from, traces, h0, h1, h3,
    matrix, first, e0, e1, e2, e3,
):
    columns = traces.shape[1]
    unknowns = got.shape[1]
    spread = []
    for i in range(2 * moves):
        source = got_s if i < moves else got
        gram = source[pl.ds(i % moves * unknowns, unknowns), :]
        scatter = moved_to[:, pl.ds(i * unknowns, unknowns)]
        spread.append(dot(scatter, gram, ((1,), (0,))).astype(BF16))
    moved = dot(jnp.concatenate(spread, axis=1), moved_from[...], ((1,), (1,)))
    whole = jnp.concatenate(halves(part[...] + moved), axis=0)
    matrix[...] = whole
    side = [
        got[pl.ds(moves * unknowns + i * fx, fx), :] for i in range(columns // unknowns)
    ]
    side = jnp.concatenate(side, axis=1)
    frame = jnp.concatenate([h0[...], h1[...], side, h3[...]], axis=0)
    field = applied(whole, traces[...], frame).astype(BF16)
    first[...] = field
    e0[...], e1[...], e2[...], e3[...] = edges_of(field, fx, fz)


def own_kernel(matrix, first, out):
    own = first.shape[0]
    both = dot(matrix[:, :own], first[...], ((1,), (0,)))
    out[...] = both[:own] + both[own:]


def second_kernel(matrix, first, h0, h1, h2, h3, out):
    own = first.shape[0]
    frame = jnp.concatenate([h0[...], h1[...], h2[...], h3[...]], axis=0)
    both = dot(matrix[:, own:], frame, ((1,), (0,)))
    out[...] = first[...] + (both[:own] + both[own:])


def pairs(count, odd):
    route = []
    for low in range(odd, count - 1, 2):
        route += [(low, low + 1), (low + 1, low)]
    return route


def swapped(edge, axis, odd):
    return lax.ppermute(edge, axis, pairs(lax.axis_size(axis), odd))


def body(
    gram_factor, coupling, order_class, first_moves, second_moves, trace_index, owner_index, traces
):
    slots, width, unknowns = coupling.shape
    moves = first_moves.shape[0]
    fx, _, fz, columns = traces.shape
    own = fx * fz
    cells = own + 2 * (fx + fz)
    most = slots - moves
    field = traces.reshape(own, columns)
    grams = jax.ShapeDtypeStruct((moves * unknowns, unknowns), BF16)
    load = jax.ShapeDtypeStruct((moves * unknowns + fx * columns // unknowns, unknowns), BF16)
    edges = [jax.ShapeDtypeStruct((n, columns), BF16) for n in (fz, fz, fx, fx)]

    def in_hbm(array):
        return pltpu.with_memory_space_constraint(array, pltpu.MemorySpace.HBM)


    def element_cost(count):
        return pl.CostEstimate(
            flops=2 * count * width * unknowns * (width + unknowns),
            bytes_accessed=2 * count * width * (width + unknowns),
            transcendentals=0,
        )

    def buffers(count):
        return [
            pltpu.VMEM((count, width, width), BF16),
            pltpu.VMEM((count, width, unknowns), BF16),
        ]

    given, t0, t1, t3 = pl.pallas_call(
        functools.partial(given_kernel, fx, fz),
        out_shape=(load, edges[0], edges[1], edges[3]),
        in_specs=[HBM] * 5,
        out_specs=(VMEM,) * 4,
        scratch_shapes=[
            pltpu.SMEM((moves,), I32),
            pltpu.SMEM((slots,), I32),
            pltpu.VMEM((own, columns), BF16),
            *buffers(moves),
            pltpu.SemaphoreType.DMA((moves, 2)),
            pltpu.SemaphoreType.DMA((3,)),
        ],
        compiler_params=params(53),
        cost_estimate=element_cost(moves),
        name="given",
    )(
        in_hbm(first_moves), in_hbm(order_class), in_hbm(gram_factor), in_hbm(coupling),
        in_hbm(field),
    )
    given, t0, t1, t3, gram_factor, coupling = lax.optimization_barrier(
        (given, t0, t1, t3, gram_factor, coupling)
    )
    got = swapped(given, "gz", 0)

    given_s, part, moved_to, moved_from, same = pl.pallas_call(
        functools.partial(kept_kernel, fx, fz),
        out_shape=(
            grams,
            jax.ShapeDtypeStruct((own, cells), F32),
            jax.ShapeDtypeStruct((own, 2 * moves * unknowns), BF16),
            jax.ShapeDtypeStruct((cells, 2 * moves * unknowns), BF16),
            jax.ShapeDtypeStruct((16 * moves * moves, unknowns), BF16),
        ),
        in_specs=[SMEM] * 3 + [VMEM] * 4,
        out_specs=(VMEM,) * 5,
        scratch_shapes=[
            pltpu.VMEM((own, most * unknowns), BF16),
            pltpu.VMEM((cells, most * unknowns), BF16),
            pltpu.VMEM((2 * own, most * unknowns), BF16),
            pltpu.VMEM((most * unknowns, unknowns), BF16),
            pltpu.VMEM((slots, unknowns), I32),
            pltpu.SMEM((slots,), I32),
        ],
        compiler_params=params(24),
        cost_estimate=element_cost(most),
        name="kept",
    )(
        first_moves, second_moves, order_class, trace_index, owner_index, gram_factor, coupling
    )

    relayed = pl.pallas_call(
        functools.partial(relay_kernel, moves),
        out_shape=grams,
        in_specs=[VMEM] * 3,
        out_specs=VMEM,
        compiler_params=params(2),
        name="relay",
    )(same, given_s, got)
    both = lax.axis_size("gy") * lax.axis_size("gz")
    second_bit = lax.axis_size("gz").bit_length() - 1
    got_s = lax.ppermute(relayed, ("gy", "gz"), swap_route(both, second_bit))
    h1 = swapped(t1, "gx", 1)
    h3 = swapped(t3, "gz", 1)
    h0 = swapped(t0, "gx", 0)

    matrix, first, *first_edges = pl.pallas_call(
        functools.partial(first_kernel, fx, fz, moves),
        out_shape=(
            jax.ShapeDtypeStruct((2 * own, cells), BF16),
            jax.ShapeDtypeStruct((own, columns), BF16),
            *edges,
        ),
        in_specs=[VMEM] * 9,
        out_specs=(VMEM,) * 6,
        compiler_params=params(12),
        name="first",
    )(got, got_s, part, moved_to, moved_from, field, h0, h1, h3)

    e0, e1, e2, e3 = first_edges
    h1 = swapped(e1, "gx", 1)
    h2 = swapped(e2, "gz", 0)
    h3 = swapped(e3, "gz", 1)
    h0 = swapped(e0, "gx", 0)
    inner = pl.pallas_call(
        own_kernel,
        out_shape=jax.ShapeDtypeStruct((own, columns), F32),
        in_specs=[VMEM] * 2,
        out_specs=VMEM,
        compiler_params=params(4),
        name="own",
    )(matrix, first)
    second = pl.pallas_call(
        second_kernel,
        out_shape=jax.ShapeDtypeStruct((own, columns), F32),
        in_specs=[VMEM] * 6,
        out_specs=VMEM,
        compiler_params=params(6),
        name="second",
    )(matrix, inner, h0, h1, h2, h3)
    return second.reshape(traces.shape)


def solution(mesh):
    return jax.shard_map(
        body,
        mesh=mesh,
        in_specs=(
            P(("gx", "gy", "gz"), None, None),
            P(("gx", "gy", "gz"), None, None),
            P(("gx", "gy", "gz")),
            P(("gx", "gy", "gz")),
            P(("gx", "gy", "gz")),
            P(("gx", "gy", "gz"), None),
            P(("gx", "gy", "gz"), None),
            P("gx", "gy", "gz", None),
        ),
        out_specs=P("gx", "gy", "gz", None),
        check_vma=False,
    )
```

```python
import functools

import jax
import jax.numpy as jnp
from jax import lax
from jax.experimental import pallas as pl
from jax.experimental.pallas import tpu as pltpu
from jax.sharding import PartitionSpec as P

BF16 = jnp.bfloat16
F32 = jnp.float32
I32 = jnp.int32
HBM = pl.BlockSpec(memory_space=pltpu.MemorySpace.HBM)
VMEM = pl.BlockSpec(memory_space=pltpu.MemorySpace.VMEM)
SMEM = pl.BlockSpec(memory_space=pltpu.MemorySpace.SMEM)


def params(mebibytes):
    return pltpu.CompilerParams(vmem_limit_bytes=int(mebibytes * 1048576))


def swap_route(count, bit):
    return [(low, low ^ (1 << bit)) for low in range(count) if low ^ (1 << bit) < count]


def dot(a, b, dims):
    return lax.dot_general(a, b, (dims, ((), ())), preferred_element_type=F32)


def halves(value):
    high = value.astype(BF16)
    return high, (value - high.astype(F32)).astype(BF16)


def grams_of(slots, order, fbuf, cbuf):
    products = [dot(fbuf[i], cbuf[i], ((1,), (0,))).astype(BF16) for i in range(len(slots))]
    operators = []
    for slot, product in zip(slots, products):
        rows = product.shape[0]
        bounds = [rows * (2 + c) // 4 for c in range(3)]
        parts = [product[: bounds[0]]]
        for c in (1, 2):
            part = product[bounds[c - 1] : bounds[c]]
            parts.append(jnp.where(order[slot] >= c, part, jnp.zeros_like(part)))
        operators.append(jnp.concatenate(parts, axis=0))
    return [dot(operator, operator, ((0,), (0,))) for operator in operators]


def one_hot(index, rows):
    tile = 16
    shape = (tile, index.shape[1])
    here = lax.broadcasted_iota(I32, shape, 0) == (index & (tile - 1))
    block = jnp.where(here, index >> 4, -1).astype(F32).astype(BF16)
    one, zero = jnp.ones(shape, BF16), jnp.zeros(shape, BF16)
    return jnp.concatenate(
        [jnp.where(block == jnp.full(shape, i, BF16), one, zero) for i in range(rows // tile)],
        axis=0,
    )


def parities():
    return lax.axis_index("gx") % 2, lax.axis_index("gz") % 2


def cell_of(cell, fx, fz):
    odd_x, odd_z = parities()
    pitch = fz + 2
    row = jnp.zeros_like(cell)
    for edge in range(1, fx + 2):
        row = row + jnp.where(cell >= edge * pitch, 1, 0)
    column = cell - row * pitch
    base_x = fx * fz
    base_z = base_x + 2 * fz
    out = (row - 1) * fz + column - 1
    out = jnp.where(column == fz + 1, base_z + odd_z * fx + row - 1, out)
    out = jnp.where(column == 0, base_z + (1 - odd_z) * fx + row - 1, out)
    out = jnp.where(row == fx + 1, base_x + odd_x * fz + column - 1, out)
    return jnp.where(row == 0, base_x + (1 - odd_x) * fz + column - 1, out)


def edges_of(field, fx, fz):
    odd_x, odd_z = parities()
    own = fx * fz
    last, first = field[own - fz :, :], field[:fz, :]
    row = lax.broadcasted_iota(I32, (2 * fx, own), 0)
    wanted = jnp.where(row < fx, row * fz + fz - 1, (row - fx) * fz)
    hit = lax.broadcasted_iota(I32, (2 * fx, own), 1) == wanted
    sides = dot(jnp.where(hit, 1.0, 0.0).astype(BF16), field, ((1,), (0,)))
    right, left = sides[:fx], sides[fx:]
    flip_x, flip_z = odd_x == 1, odd_z == 1
    return (
        jnp.where(flip_x, first, last),
        jnp.where(flip_x, last, first),
        jnp.where(flip_z, left, right).astype(BF16),
        jnp.where(flip_z, right, left).astype(BF16),
    )


def started(*copies):
    for copy in copies:
        copy.start()
    return copies


def waited(copies):
    for copy in copies:
        copy.wait()


def fetch(slots, factor, coupling, fbuf, cbuf, sem):
    copies = []
    for i, slot in enumerate(slots):
        copies += started(
            pltpu.make_async_copy(factor.at[slot], fbuf.at[i], sem.at[i, 0]),
            pltpu.make_async_copy(coupling.at[slot], cbuf.at[i], sem.at[i, 1]),
        )
    return copies


def given_kernel(
    fx, fz, f_hbm, order_hbm, factor, coupling, traces_hbm, out, e0, e1, e3,
    f, order, traces, fbuf, cbuf, sem, small,
):
    moves = f.shape[0]
    unknowns = coupling.shape[2]
    index, rest, block = started(
        pltpu.make_async_copy(f_hbm, f, small.at[0]),
        pltpu.make_async_copy(order_hbm, order, small.at[1]),
        pltpu.make_async_copy(traces_hbm, traces, small.at[2]),
    )
    index.wait()
    slots = [f[i] for i in range(moves)]
    copies = fetch(slots, factor, coupling, fbuf, cbuf, sem)
    block.wait()
    e0[...], e1[...], side, e3[...] = edges_of(traces[...], fx, fz)
    for i in range(side.shape[1] // unknowns):
        part = side[:, i * unknowns : (i + 1) * unknowns]
        out[pl.ds(moves * unknowns + i * fx, fx), :] = part
    rest.wait()
    waited(copies)
    for i, gram in enumerate(grams_of(slots, order, fbuf, cbuf)):
        out[pl.ds(i * unknowns, unknowns), :] = gram.astype(BF16)


def kept_kernel(
    fx, fz, f_from, s_from, order_from, reads, writes, factor, coupling,
    given, part, moved_to, moved_from, relayed,
    to, origin, left, grams, places, rest, f, s, order, small,
):
    slots, moves = reads.shape[0], f.shape[0]
    copies = started(
        pltpu.make_async_copy(f_from, f, small.at[0]),
        pltpu.make_async_copy(s_from, s, small.at[1]),
        pltpu.make_async_copy(order_from, order, small.at[2]),
    )
    unknowns = reads.shape[1]
    most = slots - moves
    own, cells = fx * fz, origin.shape[0]

    def among(slot, moved):
        found = moved[0] == slot
        for j in range(1, moves):
            found = found | (moved[j] == slot)
        return found

    places[...] = cell_of(reads[...], fx, fz)
    waited(copies)
    count = jnp.int32(0)
    for slot in range(slots):
        rest[count] = slot
        count = count + jnp.where(among(slot, f), 0, 1)
    wanted = [rest[i] for i in range(most)]

    def place(slot, valid, to_ref, from_ref, i):
        read = jnp.where(valid, places[pl.ds(slot, 1), :], -1)
        write = jnp.where(valid, writes[pl.ds(slot, 1), :], -1)
        columns = pl.ds(i * unknowns, unknowns)
        to_ref[:, columns] = one_hot(write, own)
        from_ref[:, columns] = one_hot(read, cells)

    tile = (16, unknowns)
    for i in range(moves):
        place(s[i], True, moved_to, moved_from, i)
        place(f[i], jnp.logical_not(among(f[i], s)), moved_to, moved_from, moves + i)
        for j in range(moves):
            same = jnp.where(s[i] == f[j], 1.0, 0.0)
            relayed[pl.ds((i * moves + j) * 16, 16), :] = jnp.full(tile, same, F32).astype(BF16)
    for i, slot in enumerate(wanted):
        place(slot, jnp.logical_not(among(slot, s)), to, origin, i)

    factors, couplings = [factor[slot] for slot in wanted], [coupling[slot] for slot in wanted]
    for i, exact in enumerate(grams_of(wanted, order, factors, couplings)):
        columns = pl.ds(i * unknowns, unknowns)
        high, low = halves(exact)
        grams[columns, :] = high
        scatter = to[:, columns]
        spread = dot(
            jnp.concatenate([scatter, scatter], axis=1),
            jnp.concatenate([high, low], axis=0),
            ((1,), (0,)),
        )
        high, low = halves(spread)
        left[:own, columns] = high
        left[own:, columns] = low
    both = dot(left[...], origin[...], ((1,), (1,)))
    part[...] = both[:own] + both[own:]
    for i in range(moves):
        at = s[i]
        for j in range(moves):
            at = at - jnp.where(f[j] < s[i], 1, 0)
        at = jnp.minimum(at, most - 1)
        source = pl.ds(pl.multiple_of(at * unknowns, unknowns), unknowns)
        given[pl.ds(i * unknowns, unknowns), :] = grams[source, :]


def relay_kernel(moves, relayed, given, got, out):
    unknowns = given.shape[0] // moves
    for i in range(moves):
        value = given[pl.ds(i * unknowns, unknowns), :]
        for j in range(moves):
            same = relayed[pl.ds((i * moves + j) * 16, 16), :]
            same = jnp.concatenate([same] * (unknowns // 16), axis=0)
            value = jnp.where(
                same > jnp.zeros_like(same), got[pl.ds(j * unknowns, unknowns), :], value
            )
        out[pl.ds(i * unknowns, unknowns), :] = value


def applied(matrix, field, frame):
    both = dot(matrix, jnp.concatenate([field, frame], axis=0), ((1,), (0,)))
    own = matrix.shape[0] // 2
    return both[:own] + both[own:]


def first_kernel(
    fx, fz, moves, got, got_s, part, moved_to, moved_from, traces, h0, h1, h3,
    matrix, first, e0, e1, e2, e3,
):
    columns = traces.shape[1]
    unknowns = got.shape[1]
    spread = []
    for i in range(2 * moves):
        source = got_s if i < moves else got
        gram = source[pl.ds(i % moves * unknowns, unknowns), :]
        scatter = moved_to[:, pl.ds(i * unknowns, unknowns)]
        spread.append(dot(scatter, gram, ((1,), (0,))).astype(BF16))
    moved = dot(jnp.concatenate(spread, axis=1), moved_from[...], ((1,), (1,)))
    whole = jnp.concatenate(halves(part[...] + moved), axis=0)
    matrix[...] = whole
    side = [
        got[pl.ds(moves * unknowns + i * fx, fx), :] for i in range(columns // unknowns)
    ]
    side = jnp.concatenate(side, axis=1)
    frame = jnp.concatenate([h0[...], h1[...], side, h3[...]], axis=0)
    field = applied(whole, traces[...], frame).astype(BF16)
    first[...] = field
    e0[...], e1[...], e2[...], e3[...] = edges_of(field, fx, fz)


def own_kernel(matrix, first, out):
    own = first.shape[0]
    both = dot(matrix[:, :own], first[...], ((1,), (0,)))
    out[...] = both[:own] + both[own:]


def second_kernel(matrix, first, h0, h1, h2, h3, out):
    own = first.shape[0]
    frame = jnp.concatenate([h0[...], h1[...], h2[...], h3[...]], axis=0)
    both = dot(matrix[:, own:], frame, ((1,), (0,)))
    out[...] = first[...] + (both[:own] + both[own:])


def pairs(count, odd):
    route = []
    for low in range(odd, count - 1, 2):
        route += [(low, low + 1), (low + 1, low)]
    return route


def swapped(edge, axis, odd):
    return lax.ppermute(edge, axis, pairs(lax.axis_size(axis), odd))


def body(
    gram_factor, coupling, order_class, first_moves, second_moves, trace_index, owner_index, traces
):
    slots, width, unknowns = coupling.shape
    moves = first_moves.shape[0]
    fx, _, fz, columns = traces.shape
    own = fx * fz
    cells = own + 2 * (fx + fz)
    most = slots - moves
    field = traces.reshape(own, columns)
    grams = jax.ShapeDtypeStruct((moves * unknowns, unknowns), BF16)
    load = jax.ShapeDtypeStruct((moves * unknowns + fx * columns // unknowns, unknowns), BF16)
    edges = [jax.ShapeDtypeStruct((n, columns), BF16) for n in (fz, fz, fx, fx)]

    def in_hbm(array):
        return pltpu.with_memory_space_constraint(array, pltpu.MemorySpace.HBM)


    def element_cost(count):
        return pl.CostEstimate(
            flops=2 * count * width * unknowns * (width + unknowns),
            bytes_accessed=2 * count * width * (width + unknowns),
            transcendentals=0,
        )

    def buffers(count):
        return [
            pltpu.VMEM((count, width, width), BF16),
            pltpu.VMEM((count, width, unknowns), BF16),
        ]

    given, t0, t1, t3 = pl.pallas_call(
        functools.partial(given_kernel, fx, fz),
        out_shape=(load, edges[0], edges[1], edges[3]),
        in_specs=[HBM] * 5,
        out_specs=(VMEM,) * 4,
        scratch_shapes=[
            pltpu.SMEM((moves,), I32),
            pltpu.SMEM((slots,), I32),
            pltpu.VMEM((own, columns), BF16),
            *buffers(moves),
            pltpu.SemaphoreType.DMA((moves, 2)),
            pltpu.SemaphoreType.DMA((3,)),
        ],
        compiler_params=params(53),
        cost_estimate=element_cost(moves),
        name="given",
    )(
        in_hbm(first_moves), in_hbm(order_class), in_hbm(gram_factor), in_hbm(coupling),
        in_hbm(field),
    )
    given, t0, t1, t3, gram_factor, coupling = lax.optimization_barrier(
        (given, t0, t1, t3, gram_factor, coupling)
    )
    got = swapped(given, "gz", 0)

    given_s, part, moved_to, moved_from, same = pl.pallas_call(
        functools.partial(kept_kernel, fx, fz),
        out_shape=(
            grams,
            jax.ShapeDtypeStruct((own, cells), F32),
            jax.ShapeDtypeStruct((own, 2 * moves * unknowns), BF16),
            jax.ShapeDtypeStruct((cells, 2 * moves * unknowns), BF16),
            jax.ShapeDtypeStruct((16 * moves * moves, unknowns), BF16),
        ),
        in_specs=[HBM] * 3 + [VMEM] * 4,
        out_specs=(VMEM,) * 5,
        scratch_shapes=[
            pltpu.VMEM((own, most * unknowns), BF16),
            pltpu.VMEM((cells, most * unknowns), BF16),
            pltpu.VMEM((2 * own, most * unknowns), BF16),
            pltpu.VMEM((most * unknowns, unknowns), BF16),
            pltpu.VMEM((slots, unknowns), I32),
            pltpu.SMEM((slots,), I32),
            pltpu.SMEM((moves,), I32),
            pltpu.SMEM((moves,), I32),
            pltpu.SMEM((slots,), I32),
            pltpu.SemaphoreType.DMA((3,)),
        ],
        compiler_params=params(24),
        cost_estimate=element_cost(most),
        name="kept",
    )(
        first_moves, second_moves, order_class, trace_index, owner_index, gram_factor, coupling
    )

    relayed = pl.pallas_call(
        functools.partial(relay_kernel, moves),
        out_shape=grams,
        in_specs=[VMEM] * 3,
        out_specs=VMEM,
        compiler_params=params(2),
        name="relay",
    )(same, given_s, got)
    both = lax.axis_size("gy") * lax.axis_size("gz")
    second_bit = lax.axis_size("gz").bit_length() - 1
    got_s = lax.ppermute(relayed, ("gy", "gz"), swap_route(both, second_bit))
    h1 = swapped(t1, "gx", 1)
    h3 = swapped(t3, "gz", 1)
    h0 = swapped(t0, "gx", 0)

    matrix, first, *first_edges = pl.pallas_call(
        functools.partial(first_kernel, fx, fz, moves),
        out_shape=(
            jax.ShapeDtypeStruct((2 * own, cells), BF16),
            jax.ShapeDtypeStruct((own, columns), BF16),
            *edges,
        ),
        in_specs=[VMEM] * 9,
        out_specs=(VMEM,) * 6,
        compiler_params=params(12),
        name="first",
    )(got, got_s, part, moved_to, moved_from, field, h0, h1, h3)

    e0, e1, e2, e3 = first_edges
    h1 = swapped(e1, "gx", 1)
    h2 = swapped(e2, "gz", 0)
    h3 = swapped(e3, "gz", 1)
    h0 = swapped(e0, "gx", 0)
    inner = pl.pallas_call(
        own_kernel,
        out_shape=jax.ShapeDtypeStruct((own, columns), F32),
        in_specs=[VMEM] * 2,
        out_specs=VMEM,
        compiler_params=params(4),
        name="own",
    )(matrix, first)
    second = pl.pallas_call(
        second_kernel,
        out_shape=jax.ShapeDtypeStruct((own, columns), F32),
        in_specs=[VMEM] * 6,
        out_specs=VMEM,
        compiler_params=params(6),
        name="second",
    )(matrix, inner, h0, h1, h2, h3)
    return second.reshape(traces.shape)


def solution(mesh):
    return jax.shard_map(
        body,
        mesh=mesh,
        in_specs=(
            P(("gx", "gy", "gz"), None, None),
            P(("gx", "gy", "gz"), None, None),
            P(("gx", "gy", "gz")),
            P(("gx", "gy", "gz")),
            P(("gx", "gy", "gz")),
            P(("gx", "gy", "gz"), None),
            P(("gx", "gy", "gz"), None),
            P("gx", "gy", "gz", None),
        ),
        out_specs=P("gx", "gy", "gz", None),
        check_vma=False,
    )
```
